32 devices in a mesh: img: 8 (over y, x, core), seq: 4 (over z).
Axes of the slice: x: 2, y: 2, z: 4, core: 2. Of those that a mesh axis runs over, the one named last changes fastest.
Arguments:
- x_big: bfloat16 [128, 200, 768], P(('img', 'seq')), may hold values from -6 to 6
- x_small: bfloat16 [512, 40, 768], P(('img', 'seq')), may hold values from -6 to 6
- mask_big: int32 [128, 200], P('img'), may hold values from 0 to 1, as said below
- mask_small: int32 [512, 40], P('img'), may hold values from 0 to 1, as said below
- ln1_gain: float32 [768], P('seq'), may hold values from 0.5 to 1.5
- ln1_bias: float32 [768], P('seq'), may hold values from -1.75 to 1.75
- w_qkv: float32 [768, 2304], P('img', 'seq'), may hold values from -0.21875 to 0.21875
- b_qv: float32 [1536], P('seq'), may hold values from -3 to 3
- w_out: float32 [768, 768], P('img', 'seq'), may hold values from -0.625 to 0.625
- b_out: float32 [768], P('seq'), may hold values from -1.75 to 1.75
- ln2_gain: float32 [768], P('seq'), may hold values from 0.5 to 1.5
- ln2_bias: float32 [768], P('seq'), may hold values from -1.75 to 1.75
- w_up: float32 [768, 3072], P('img', 'seq'), may hold values from -0.21875 to 0.21875
- b_up: float32 [3072], P('seq'), may hold values from -3 to 3
- w_down: float32 [3072, 768], P('img', 'seq'), may hold values from -0.109375 to 0.109375
- b_down: float32 [768], P('seq'), may hold values from -1.75 to 1.75
- dy_big: bfloat16 [128, 200, 768], P(('img', 'seq')), may hold values from -6 to 6
- dy_small: bfloat16 [512, 40, 768], P(('img', 'seq')), may hold values from -6 to 6
Outputs:
- y_big: bfloat16 [128, 200, 768], P(('img', 'seq'))
- y_small: bfloat16 [512, 40, 768], P(('img', 'seq'))
- dx_big: bfloat16 [128, 200, 768], P(('img', 'seq'))
- dx_small: bfloat16 [512, 40, 768], P(('img', 'seq'))
- g_ln1_gain: float32 [768], P('seq')
- g_ln1_bias: float32 [768], P('seq')
- g_w_qkv: float32 [768, 2304], P('img', 'seq')
- g_b_qv: float32 [1536], P('seq')
- g_w_out: float32 [768, 768], P('img', 'seq')
- g_b_out: float32 [768], P('seq')
- g_ln2_gain: float32 [768], P('seq')
- g_ln2_bias: float32 [768], P('seq')
- g_w_up: float32 [768, 3072], P('img', 'seq')
- g_b_up: float32 [3072], P('seq')
- g_w_down: float32 [3072, 768], P('img', 'seq')
- g_b_down: float32 [768], P('seq')
The draws below stay inside these ranges and needn't reach their ends.
Inputs may be any that keep to these rules, and one draw needn't show every extreme that they name: `mask_big`: each 224px crop's mask is 1 on its first 175 to 200 slots and 0 after; some crop has all slots valid and some the fewest. `mask_small`: each 96px crop's mask is 1 on its first 35 to 40 slots and 0 after; some crop has all slots valid and some the fewest.
All inputs are finite; a program needn't handle non-finite values.
Results may differ from the reference program's by a relative error of at most 0.014.
Values may be sent and summed in bfloat16 or wider, within the bound.
A program may use at most 192 MiB of HBM per device.

```python
from functools import partial
import jax
import jax.numpy as jnp
from jax import lax

D = 768
FF = 3072
HEADS = 12
HEAD_DIM = 64
LB = 200
LS = 40
BIGCROPS = 128
SMALLCROPS = 512


def prefix_mask(key, crop_count, length):
    fewest = length - length // 8
    counts = jax.random.randint(key, (crop_count,), fewest, length + 1)
    counts = counts.at[0].set(fewest).at[1].set(length)
    positions = jnp.arange(length)
    return (positions[None, :] < counts[:, None]).astype(jnp.int32)


def draw_mask_big(key, part):
    return prefix_mask(jax.random.fold_in(key, 11), BIGCROPS, LB)


def draw_mask_small(key, part):
    return prefix_mask(jax.random.fold_in(key, 23), SMALLCROPS, LS)


def spiked(drawn, key, source, target, shards_of, factor):
    owner, partner = [(jnp.arange(drawn.shape[axis_at]) // (drawn.shape[axis_at] // shards_of)).reshape([-1 if axis == axis_at else 1 for axis in range(drawn.ndim)]) for axis_at in (source, target)]
    chosen = jax.random.permutation(key, shards_of)[partner]
    strong = (owner == chosen) | (owner == (partner + shards_of // 2) % shards_of)
    return jnp.where(strong, factor * drawn, drawn)


def level_of(rng, shape, split, least, top_value):
    level, own = 1.0, jax.random.fold_in(rng, 6)
    for dim, parts in split:
        steps = jnp.exp(jax.random.uniform(jax.random.fold_in(own, dim), (parts,), jnp.float32, least / len(split), top_value / len(split)))
        level = level * jnp.repeat(steps, shape[dim] // parts).reshape([-1 if axis == dim else 1 for axis in range(len(shape))])
    return level


def normal_values(stream_key, extent, spread, most, shards=(), kind=jnp.bfloat16):
    values = spread * jax.random.normal(stream_key, extent, jnp.float32)
    if shards:
        values = values * level_of(stream_key, extent, shards, -0.22, 0.18)
    return jnp.clip(values, -most, most).astype(kind)


def noise_with(own_key, shape, spread, most, shards, heavy, dtype=jnp.bfloat16):
    values = spread * jax.random.normal(own_key, shape, jnp.float32)
    if shards:
        values = values * level_of(own_key, shape, shards, -0.22, 0.18)
    return jnp.clip(spiked(values, jax.random.fold_in(own_key, 3), *heavy), -most, most).astype(dtype)


def setup_inputs(seed: int = 0) -> dict:
    seeds = jax.random.split(jax.random.key(seed), 19)
    x_big = noise_with(seeds[0], (BIGCROPS, LB, D), 1.0, 6.0, ((0, 32),), (0, 2, 32, 2.75))
    x_small = noise_with(seeds[1], (SMALLCROPS, LS, D), 1.0, 6.0, ((0, 32),), (0, 2, 32, 2.75))
    mask_big = draw_mask_big(jax.random.fold_in(seeds[18], 71), 0)
    mask_small = draw_mask_small(jax.random.fold_in(seeds[18], 71), 0)
    ln1_gain = jnp.clip(1.0 + 0.1 * jax.random.normal(seeds[4], (D,), jnp.float32), 0.5, 1.5)
    ln1_bias = normal_values(seeds[5], (D,), 0.3, 1.75, ((0, 4),), jnp.float32)
    w_qkv = normal_values(seeds[6], (D, 3 * D), D ** -0.5, 0.21875, ((0, 8), (1, 4)), jnp.float32)
    b_qv = normal_values(seeds[7], (2 * D,), 0.5, 3.0, ((0, 4),), jnp.float32)
    w_out = normal_values(seeds[8], (D, D), (D // 8) ** -0.5, 0.625, ((0, 8), (1, 4)), jnp.float32)
    b_out = normal_values(seeds[9], (D,), 0.3, 1.75, ((0, 4),), jnp.float32)
    ln2_gain = jnp.clip(1.0 + 0.1 * jax.random.normal(seeds[10], (D,), jnp.float32), 0.5, 1.5)
    ln2_bias = normal_values(seeds[11], (D,), 0.3, 1.75, ((0, 4),), jnp.float32)
    w_up = normal_values(seeds[12], (D, FF), D ** -0.5, 0.21875, ((0, 8), (1, 4)), jnp.float32)
    b_up = normal_values(seeds[13], (FF,), 0.5, 3.0, ((0, 4),), jnp.float32)
    w_down = normal_values(seeds[14], (FF, D), FF ** -0.5, 0.109375, ((0, 8), (1, 4)), jnp.float32)
    b_down = normal_values(seeds[15], (D,), 0.3, 1.75, ((0, 4),), jnp.float32)
    dy_big = normal_values(seeds[16], (BIGCROPS, LB, D), 1.0, 6.0, ((0, 32),))
    dy_small = normal_values(seeds[17], (SMALLCROPS, LS, D), 1.0, 6.0, ((0, 32),))
    return {"x_big": x_big, "x_small": x_small, "mask_big": mask_big, "mask_small": mask_small, "ln1_gain": ln1_gain, "ln1_bias": ln1_bias, "w_qkv": w_qkv, "b_qv": b_qv, "w_out": w_out, "b_out": b_out, "ln2_gain": ln2_gain, "ln2_bias": ln2_bias, "w_up": w_up, "b_up": b_up, "w_down": w_down, "b_down": b_down, "dy_big": dy_big, "dy_small": dy_small}


EPSILON = 1e-06
NEGATIVE = -1e+30
HIGH = lax.Precision.HIGHEST

@jax.custom_vjp
def low(v):
    return lax.optimization_barrier(v.astype(jnp.bfloat16)).astype(jnp.float32)

@jax.custom_vjp
def low_back(v):
    return v

def low_keep(v):
    return (low(v), None)

def low_pass(kept, grad):
    return (grad,)

def back_keep(v):
    return (v, None)

def back_low(kept, grad):
    return (low(grad),)
low.defvjp(low_keep, low_pass)
low_back.defvjp(back_keep, back_low)

def layer_norm(values, gain_vec, shift_vec):
    row_mean = lax.optimization_barrier(jnp.mean(values, axis=-1, keepdims=True))
    centred = values - row_mean
    variance = lax.optimization_barrier(jnp.mean(centred * centred, axis=-1, keepdims=True))
    return centred * lax.rsqrt(variance + EPSILON) * gain_vec + shift_vec

def gelu_exact(values):
    return jax.nn.gelu(values, approximate=False)

def attend_crop(queries, key_rows, value_rows, key_valid):
    raw_scores = low_back(jnp.einsum('qhd,khd->hqk', queries, key_rows, precision=HIGH))
    scores = jnp.where(key_valid[None, None, :] > 0, raw_scores * HEAD_DIM ** (-0.5), NEGATIVE)
    row_max = lax.optimization_barrier(jnp.max(scores, axis=-1, keepdims=True))
    exponent = jnp.exp(scores - row_max)
    softmax_w = exponent / lax.optimization_barrier(jnp.sum(exponent, axis=-1, keepdims=True))
    return jnp.einsum('hqk,khd->qhd', low(softmax_w), value_rows, precision=HIGH)

def attend_group(projected, key_mask, crop_count, length):
    pieces = projected.reshape(crop_count, length, 3, HEADS, HEAD_DIM)
    per_crop = jax.checkpoint(attend_crop)
    mixed_out = lax.map(lambda crop_items: per_crop(crop_items[0], crop_items[1], crop_items[2], crop_items[3]), (pieces[:, :, 0], pieces[:, :, 1], pieces[:, :, 2], key_mask))
    return mixed_out.reshape(crop_count * length, HEADS * HEAD_DIM)

def forward(mask_big, mask_small, x_big, x_small, ln1_gain, ln1_bias, w_qkv, b_qv, w_out, b_out, ln2_gain, ln2_bias, w_up, b_up, w_down, b_down):
    model_width = HEADS * HEAD_DIM
    big_rows = BIGCROPS * LB
    tokens = jnp.concatenate([x_big.reshape(big_rows, model_width), x_small.reshape(SMALLCROPS * LS, model_width)], axis=0)
    normed_one = low(layer_norm(tokens, low(ln1_gain), low(ln1_bias)))
    bias_qv = low(b_qv)
    bias_qkv = jnp.concatenate([bias_qv[:model_width], jnp.zeros((model_width,), jnp.float32), bias_qv[model_width:]])
    projected = low_back(low(jnp.dot(normed_one, low(w_qkv), precision=HIGH) + bias_qkv))
    mixed_out = jnp.concatenate([attend_group(projected[:big_rows], mask_big, BIGCROPS, LB), attend_group(projected[big_rows:], mask_small, SMALLCROPS, LS)], axis=0)
    mixed_out = low_back(low(mixed_out))
    branch = low_back(jnp.dot(mixed_out, low(w_out), precision=HIGH) + low(b_out))
    middle = tokens + branch
    normed_two = low(layer_norm(middle, low(ln2_gain), low(ln2_bias)))
    up_proj = low_back(jnp.dot(normed_two, low(w_up), precision=HIGH) + low(b_up))
    activated = low(gelu_exact(up_proj))
    result = middle + jnp.dot(activated, low(w_down), precision=HIGH) + low(b_down)
    return (result[:big_rows].reshape(BIGCROPS, LB, model_width), result[big_rows:].reshape(SMALLCROPS, LS, model_width))

def reference(x_big, x_small, mask_big, mask_small, ln1_gain, ln1_bias, w_qkv, b_qv, w_out, b_out, ln2_gain, ln2_bias, w_up, b_up, w_down, b_down, dy_big, dy_small):
    floats = [arr.astype(jnp.float32) for arr in (x_big, x_small, ln1_gain, ln1_bias, w_qkv, b_qv, w_out, b_out, ln2_gain, ln2_bias, w_up, b_up, w_down, b_down)]
    outputs, pull = jax.vjp(partial(forward, mask_big, mask_small), *floats)
    grads = pull((dy_big.astype(jnp.float32), dy_small.astype(jnp.float32)))
    return (outputs[0].astype(jnp.bfloat16), outputs[1].astype(jnp.bfloat16), grads[0].astype(jnp.bfloat16), grads[1].astype(jnp.bfloat16), grads[2], grads[3], grads[4], grads[5], grads[6], grads[7], grads[8], grads[9], grads[10], grads[11], grads[12], grads[13])
```

```python
import jax
import jax.numpy as jnp
from jax import lax
from jax.sharding import PartitionSpec as P

HEADS = 12
HEAD_DIM = 64
AXES = ("img", "seq")

EPSILON = 1e-06
NEGATIVE = -1e30


def layer_norm(values, gain_vec, shift_vec):
    row_mean = jnp.mean(values, axis=-1, keepdims=True)
    centred = values - row_mean
    variance = jnp.mean(centred * centred, axis=-1, keepdims=True)
    return centred * lax.rsqrt(variance + EPSILON) * gain_vec + shift_vec


def gelu_exact(values):
    return jax.nn.gelu(values, approximate=False)


def head_scores(heads_in, key_valid):
    crop_count, length = (heads_in.shape[0], heads_in.shape[1])
    pieces = heads_in.reshape(crop_count, length, 3, HEADS, HEAD_DIM)
    queries, key_rows, value_rows = (pieces[:, :, 0], pieces[:, :, 1], pieces[:, :, 2])
    raw_scores = jnp.einsum(
        "cqhd,ckhd->chqk", queries, key_rows, preferred_element_type=jnp.float32
    )
    scores = jnp.where(key_valid[:, None, None, :] > 0, raw_scores * HEAD_DIM ** (-0.5), NEGATIVE)
    return (queries, key_rows, value_rows, scores)


def attend(heads_in, key_valid):
    crop_count, length = (heads_in.shape[0], heads_in.shape[1])
    queries, key_rows, value_rows, scores = head_scores(heads_in, key_valid)
    row_max = jnp.max(scores, axis=-1, keepdims=True)
    exponent = jnp.exp(scores - row_max)
    row_total = jnp.sum(exponent, axis=-1, keepdims=True)
    softmax_w = (exponent / row_total).astype(jnp.bfloat16)
    mixed_out = jnp.einsum(
        "chqk,ckhd->cqhd", softmax_w, value_rows, preferred_element_type=jnp.float32
    )
    log_total = row_max + jnp.log(row_total)
    return (mixed_out.astype(jnp.bfloat16).reshape(crop_count * length, -1), log_total)


def attend_back(heads_in, key_valid, log_total, grad_heads):
    crop_count, length = (heads_in.shape[0], heads_in.shape[1])
    queries, key_rows, value_rows, scores = head_scores(heads_in, key_valid)
    softmax_f = jnp.exp(scores - log_total)
    grad_mixed = grad_heads.reshape(crop_count, length, HEADS, HEAD_DIM)
    grad_soft = jnp.einsum(
        "cqhd,ckhd->chqk", grad_mixed, value_rows, preferred_element_type=jnp.float32
    )
    inner_sum = jnp.sum(softmax_f * grad_soft, axis=-1, keepdims=True)
    grad_raw = (softmax_f * (grad_soft - inner_sum) * HEAD_DIM ** (-0.5)).astype(jnp.bfloat16)
    grad_query = jnp.einsum(
        "chqk,ckhd->cqhd", grad_raw, key_rows, preferred_element_type=jnp.float32
    )
    grad_key = jnp.einsum("chqk,cqhd->ckhd", grad_raw, queries, preferred_element_type=jnp.float32)
    grad_value = jnp.einsum(
        "chqk,cqhd->ckhd",
        softmax_f.astype(jnp.bfloat16),
        grad_mixed,
        preferred_element_type=jnp.float32,
    )
    stacked = jnp.stack([grad_query, grad_key, grad_value], axis=2).astype(jnp.bfloat16)
    return stacked.reshape(crop_count * length, -1)


def gather_mats(mats):
    n_img, n_seq = lax.axis_size("img"), lax.axis_size("seq")
    flat = jnp.concatenate([m.astype(jnp.bfloat16).reshape(-1, 64) for m in mats], axis=0)
    whole = lax.all_gather(flat, AXES, axis=0, tiled=False)
    outs, at = [], 0
    for m in mats:
        rows = m.size // 64
        piece = whole[:, at : at + rows].reshape((n_img, n_seq) + m.shape)
        at += rows
        if m.ndim == 2:
            piece = piece.transpose(0, 2, 1, 3).reshape(n_img * m.shape[0], n_seq * m.shape[1])
        else:
            piece = piece[0].reshape(-1)
        outs.append(piece)
    return outs


def scatter_mats(mats):
    n_img, n_seq = lax.axis_size("img"), lax.axis_size("seq")
    blocks = []
    for m in mats:
        rows, cols = m.shape[0] // n_img, m.shape[1] // n_seq
        b = m.astype(jnp.bfloat16).reshape(n_img, rows, n_seq, cols).transpose(0, 2, 1, 3)
        blocks.append(b.reshape(n_img * n_seq, -1, 128))
    flat = jnp.concatenate(blocks, axis=1)
    mine = lax.psum_scatter(flat, AXES, scatter_dimension=0, tiled=False)
    outs, at = [], 0
    for m, b in zip(mats, blocks):
        piece = mine[at : at + b.shape[1]]
        at += b.shape[1]
        outs.append(piece.reshape(m.shape[0] // n_img, m.shape[1] // n_seq).astype(jnp.float32))
    return outs


def body(
    x_big,
    x_small,
    mask_big,
    mask_small,
    ln1_gain,
    ln1_bias,
    w_qkv,
    b_qv,
    w_out,
    b_out,
    ln2_gain,
    ln2_bias,
    w_up,
    b_up,
    w_down,
    b_down,
    dy_big,
    dy_small,
):
    n_seq = lax.axis_size("seq")
    where = lax.axis_index("seq")
    model_width = x_big.shape[2]
    big_crops, big_length = (x_big.shape[0], x_big.shape[1])
    small_crops, small_length = (x_small.shape[0], x_small.shape[1])
    big_rows = big_crops * big_length
    mask_big = lax.dynamic_slice_in_dim(mask_big, where * big_crops, big_crops, 0)
    mask_small = lax.dynamic_slice_in_dim(mask_small, where * small_crops, small_crops, 0)
    (
        qkv_full,
        gain_one,
        shift_one,
        bias_qv,
        bias_out,
        gain_two,
        shift_two,
        bias_up,
        bias_down,
    ) = gather_mats([w_qkv, ln1_gain, ln1_bias, b_qv, b_out, ln2_gain, ln2_bias, b_up, b_down])
    out_full, up_full, down_full = gather_mats([w_out, w_up, w_down])
    gain_one, shift_one, bias_qv, bias_out, gain_two, shift_two, bias_up, bias_down = tuple(
        (
            vec.astype(jnp.float32)
            for vec in (
                gain_one,
                shift_one,
                bias_qv,
                bias_out,
                gain_two,
                shift_two,
                bias_up,
                bias_down,
            )
        )
    )
    tokens = jnp.concatenate(
        [x_big.reshape(big_rows, model_width), x_small.reshape(-1, model_width)], axis=0
    ).astype(jnp.float32)
    normed_one, pull_one = jax.vjp(layer_norm, tokens, gain_one, shift_one)
    input_one = normed_one.astype(jnp.bfloat16)
    bias_qkv = jnp.concatenate(
        [bias_qv[:model_width], jnp.zeros((model_width,), jnp.float32), bias_qv[model_width:]]
    )
    projected = (
        jnp.dot(input_one, qkv_full, preferred_element_type=jnp.float32) + bias_qkv
    ).astype(jnp.bfloat16)
    heads_big = projected[:big_rows].reshape(big_crops, big_length, -1)
    heads_small = projected[big_rows:].reshape(small_crops, small_length, -1)
    mixed_big, total_big = attend(heads_big, mask_big)
    mixed_small, total_small = attend(heads_small, mask_small)
    mixed_tok = jnp.concatenate([mixed_big, mixed_small], axis=0)
    middle = tokens + jnp.dot(mixed_tok, out_full, preferred_element_type=jnp.float32) + bias_out
    normed_two, pull_two = jax.vjp(layer_norm, middle, gain_two, shift_two)
    input_two = normed_two.astype(jnp.bfloat16)
    up_proj = jnp.dot(input_two, up_full, preferred_element_type=jnp.float32) + bias_up
    activated_f, pull_act = jax.vjp(gelu_exact, up_proj)
    activated = activated_f.astype(jnp.bfloat16)
    result = middle + jnp.dot(activated, down_full, preferred_element_type=jnp.float32) + bias_down
    grad_out = jnp.concatenate(
        [dy_big.reshape(big_rows, model_width), dy_small.reshape(-1, model_width)], axis=0
    )
    grad_down = jnp.einsum("ti,tj->ij", activated, grad_out, preferred_element_type=jnp.float32)
    grad_bias_down = jnp.sum(grad_out.astype(jnp.float32), axis=0)
    grad_act = jnp.einsum("tj,ij->ti", grad_out, down_full, preferred_element_type=jnp.float32)
    (grad_up_f,) = pull_act(grad_act)
    grad_up_b = grad_up_f.astype(jnp.bfloat16)
    grad_upw = jnp.einsum("ti,tj->ij", input_two, grad_up_b, preferred_element_type=jnp.float32)
    grad_bias_up = jnp.sum(grad_up_b.astype(jnp.float32), axis=0)
    grad_in_two = jnp.einsum("tj,ij->ti", grad_up_b, up_full, preferred_element_type=jnp.float32)
    grad_middle_ln, grad_gain_two, grad_shift_two = pull_two(grad_in_two)
    grad_middle = grad_out.astype(jnp.float32) + grad_middle_ln
    grad_branch = grad_middle.astype(jnp.bfloat16)
    grad_bias_out = jnp.sum(grad_branch.astype(jnp.float32), axis=0)
    grad_outw = jnp.einsum("ti,tj->ij", mixed_tok, grad_branch, preferred_element_type=jnp.float32)
    grad_mixed = jnp.einsum(
        "tj,ij->ti", grad_branch, out_full, preferred_element_type=jnp.float32
    ).astype(jnp.bfloat16)
    grad_projected = jnp.concatenate(
        [
            attend_back(heads_big, mask_big, total_big, grad_mixed[:big_rows]),
            attend_back(heads_small, mask_small, total_small, grad_mixed[big_rows:]),
        ],
        axis=0,
    )
    grad_qkvw = jnp.einsum(
        "ti,tj->ij", input_one, grad_projected, preferred_element_type=jnp.float32
    )
    grad_proj_sums = jnp.sum(grad_projected.astype(jnp.float32), axis=0)
    grad_bias_qv = jnp.concatenate(
        [grad_proj_sums[:model_width], grad_proj_sums[2 * model_width :]]
    )
    grad_in_one = jnp.einsum(
        "tj,ij->ti", grad_projected, qkv_full, preferred_element_type=jnp.float32
    )
    grad_tokens_ln, grad_gain_one, grad_shift_one = pull_one(grad_in_one)
    grad_tokens = (grad_middle + grad_tokens_ln).astype(jnp.bfloat16)
    vectors = (
        grad_gain_one,
        grad_shift_one,
        grad_bias_qv,
        grad_bias_out,
        grad_gain_two,
        grad_shift_two,
        grad_bias_up,
        grad_bias_down,
    )
    vector_sums = lax.psum(jnp.concatenate(vectors), AXES)
    vec_out, at = [], 0
    for v in vectors:
        width = v.shape[0] // n_seq
        vec_out.append(lax.dynamic_slice(vector_sums, (at + where * width,), (width,)))
        at += v.shape[0]
    g_up, g_down = scatter_mats([grad_upw, grad_down])
    g_qkv, g_out = scatter_mats([grad_qkvw, grad_outw])
    y_big = result[:big_rows].reshape(big_crops, big_length, model_width).astype(jnp.bfloat16)
    y_small = result[big_rows:].reshape(small_crops, small_length, model_width).astype(jnp.bfloat16)
    dx_big = grad_tokens[:big_rows].reshape(big_crops, big_length, model_width)
    dx_small = grad_tokens[big_rows:].reshape(small_crops, small_length, model_width)
    return (
        y_big,
        y_small,
        dx_big,
        dx_small,
        vec_out[0],
        vec_out[1],
        g_qkv,
        vec_out[2],
        g_out,
        vec_out[3],
        vec_out[4],
        vec_out[5],
        g_up,
        vec_out[6],
        g_down,
        vec_out[7],
    )


def solution(mesh):
    rows3 = P(AXES, None, None)
    placed = (
        rows3,
        rows3,
        P("img", None),
        P("img", None),
        P("seq"),
        P("seq"),
        P("img", "seq"),
        P("seq"),
        P("img", "seq"),
        P("seq"),
        P("seq"),
        P("seq"),
        P("img", "seq"),
        P("seq"),
        P("img", "seq"),
        P("seq"),
        rows3,
        rows3,
    )
    return jax.shard_map(
        body,
        mesh=mesh,
        in_specs=placed,
        out_specs=(rows3,) * 4
        + (
            P("seq"),
            P("seq"),
            P("img", "seq"),
            P("seq"),
            P("img", "seq"),
            P("seq"),
            P("seq"),
            P("seq"),
            P("img", "seq"),
            P("seq"),
            P("img", "seq"),
            P("seq"),
        ),
        check_vma=False,
    )
```
